32 devices in a mesh: dp: 2 (over x), sp: 4 (over y, core), tp: 4 (over z).
Axes of the slice: x: 2, y: 2, z: 4, core: 2. Of those that a mesh axis runs over, the one named last changes fastest.
Arguments:
- inputs: bfloat16 [2, 1536, 2048], P('dp', 'sp'), may hold values from -6 to 6
- w_query: bfloat16 [2048, 2048], P(None, 'tp'), may hold values from -2 to 2
- w_key: bfloat16 [2048, 2048], P(None, 'tp'), may hold values from -2 to 2
- w_value: bfloat16 [2048, 2048], P(None, 'tp'), may hold values from -0.125 to 0.125
- w_out: bfloat16 [2048, 2048], P('tp'), may hold values from -0.125 to 0.125
- w_gate: bfloat16 [2048, 8192], P(None, 'tp'), may hold values from -0.125 to 0.125
- w_up: bfloat16 [2048, 8192], P(None, 'tp'), may hold values from -0.125 to 0.125
- w_down: bfloat16 [8192, 2048], P('tp'), may hold values from -0.0625 to 0.0625
- q_gain: float32 [2048], P('tp'), may hold values from 0.6 to 1.6
- k_gain: float32 [2048], P('tp'), may hold values from 0.6 to 1.6
- attn_gain: float32 [2048], replicated, may hold values from 0.1 to 1.9
- mlp_gain: float32 [2048], replicated, may hold values from 0.1 to 1.9
- out_grad: bfloat16 [2, 1536, 2048], P('dp', 'sp'), may hold values from -6 to 6
Outputs:
- output: bfloat16 [2, 1536, 2048], P('dp', 'sp')
- input_grad: float32 [2, 1536, 2048], P('dp', 'sp')
- w_query_grad: float32 [2048, 2048], P(('dp', 'sp'), 'tp')
- w_key_grad: float32 [2048, 2048], P(('dp', 'sp'), 'tp')
- w_value_grad: float32 [2048, 2048], P(('dp', 'sp'), 'tp')
- w_out_grad: float32 [2048, 2048], P('tp', ('dp', 'sp'))
- w_gate_grad: float32 [2048, 8192], P(('dp', 'sp'), 'tp')
- w_up_grad: float32 [2048, 8192], P(('dp', 'sp'), 'tp')
- w_down_grad: float32 [8192, 2048], P('tp', ('dp', 'sp'))
- q_gain_grad: float32 [2048], P('tp')
- k_gain_grad: float32 [2048], P('tp')
- attn_gain_grad: float32 [2048], P(('dp', 'sp'))
- mlp_gain_grad: float32 [2048], P(('dp', 'sp'))
The draws below stay inside these ranges and needn't reach their ends.
All inputs are finite; a program needn't handle non-finite values.
Results may differ from the reference program's by a relative error of at most 0.018.
Values may be sent and summed in bfloat16 or wider, within the bound.
No kernel may reach another device: no remote copies, remote signals or barrier semaphores. Data moves between devices by JAX's collectives and lax.ppermute only.
A program may use at most 256 MiB of HBM per device.

```python
import jax
import jax.numpy as jnp
from jax import lax

D = 2048
HEADS = 16
HD = 128
FF = 8192
SEQ = 1536
SEQS = 2


def projection(key):
    base = jax.random.normal(key, (D, D), jnp.float32) * D ** (-0.5)
    column = (jnp.arange(D) // HD).astype(jnp.float32)
    factor = 3.0 ** (column / (HEADS - 1))
    return jnp.clip(base * factor[None, :], -2.0, 2.0).astype(jnp.bfloat16)


def score_gain(key):
    return jax.random.uniform(key, (D,), jnp.float32, 0.6, 1.6)


def draw_w_query(key, part):
    return projection(jax.random.fold_in(key, 11))


def draw_w_key(key, part):
    return projection(jax.random.fold_in(key, 12))


def draw_q_gain(key, part):
    return score_gain(jax.random.fold_in(key, 21))


def draw_k_gain(key, part):
    return score_gain(jax.random.fold_in(key, 22))


def block_levels(stream_key, extent, split, least, high):
    level, own = 1.0, jax.random.fold_in(stream_key, 6)
    for dim, blocks in split:
        draws = jnp.exp(jax.random.uniform(jax.random.fold_in(own, dim), (blocks,), jnp.float32, least / len(split), high / len(split)))
        level = level * jnp.repeat(draws, extent[dim] // blocks).reshape([-1 if axis == dim else 1 for axis in range(len(extent))])
    return level


def noise(rng, extent, scale, most, shards=(), kind=jnp.bfloat16):
    values = scale * jax.random.normal(rng, extent, jnp.float32)
    if shards:
        values = values * block_levels(rng, extent, shards, -0.22, 0.18)
    return jnp.clip(values, -most, most).astype(kind)


def setup_inputs(seed: int = 0) -> dict:
    key_list = jax.random.split(jax.random.key(seed), 14)
    inputs = noise(key_list[0], (SEQS, SEQ, D), 1.0, 6.0, ((0, 2), (1, 4)))
    w_query = draw_w_query(jax.random.fold_in(key_list[13], 71), 0)
    w_key = draw_w_key(jax.random.fold_in(key_list[13], 71), 0)
    w_value = noise(key_list[3], (D, D), D ** -0.5, 0.125, ((1, 4),))
    w_out = noise(key_list[4], (D, D), D ** -0.5, 0.125, ((0, 4),))
    w_gate = noise(key_list[5], (D, FF), D ** -0.5, 0.125, ((1, 4),))
    w_up = noise(key_list[6], (D, FF), D ** -0.5, 0.125, ((1, 4),))
    w_down = noise(key_list[7], (FF, D), FF ** -0.5, 0.0625, ((0, 4),))
    q_gain = draw_q_gain(jax.random.fold_in(key_list[13], 71), 0)
    k_gain = draw_k_gain(jax.random.fold_in(key_list[13], 71), 0)
    attn_gain = jnp.clip(1.0 + 0.18 * jax.random.normal(key_list[10], (D,), jnp.float32), 0.1, 1.9)
    mlp_gain = jnp.clip(1.0 + 0.18 * jax.random.normal(key_list[11], (D,), jnp.float32), 0.1, 1.9)
    out_grad = noise(key_list[12], (SEQS, SEQ, D), 1.0, 6.0, ((0, 2), (1, 4)))
    return {"inputs": inputs, "w_query": w_query, "w_key": w_key, "w_value": w_value, "w_out": w_out, "w_gate": w_gate, "w_up": w_up, "w_down": w_down, "q_gain": q_gain, "k_gain": k_gain, "attn_gain": attn_gain, "mlp_gain": mlp_gain, "out_grad": out_grad}


EPSILON = 1e-06
THETA = 500000.0

@jax.custom_vjp
def low(v):
    return lax.optimization_barrier(v.astype(jnp.bfloat16)).astype(jnp.float32)

@jax.custom_vjp
def low_back(v):
    return v

def low_keep(v):
    return (low(v), None)

def low_pass(kept, grad):
    return (grad,)

def back_keep(v):
    return (v, None)

def back_low(kept, grad):
    return (low(grad),)
low.defvjp(low_keep, low_pass)
low_back.defvjp(back_keep, back_low)

def dense(left, right):
    return jnp.dot(left, right, precision=lax.Precision.HIGHEST, preferred_element_type=jnp.float32)

def rms_norm(field, gain):
    return field * lax.rsqrt(lax.optimization_barrier(jnp.mean(field * field, axis=-1, keepdims=True)) + EPSILON) * gain

def rope_tables(length):
    half = HD // 2
    freq = 1.0 / THETA ** (jnp.arange(half, dtype=jnp.float32) * 2.0 / HD)
    angle = jnp.arange(length).astype(jnp.float32)[:, None] * freq[None, :]
    return (jnp.cos(angle)[:, None, :], jnp.sin(angle)[:, None, :])

def rotate(field, cosine, sine):
    half = field.shape[-1] // 2
    first = field[..., :half]
    second = field[..., half:]
    return jnp.concatenate([first * cosine - second * sine, second * cosine + first * sine], axis=-1)

def head_attend(items):
    query_head, key_head, value_head = items
    length = query_head.shape[0]
    scores = low_back(dense(query_head, key_head.T) * HD ** (-0.5))
    allowed = jnp.arange(length)[None, :] <= jnp.arange(length)[:, None]
    probs = jax.nn.softmax(jnp.where(allowed, scores, -jnp.inf), axis=-1)
    return dense(low(probs), value_head)

def forward(tokens, w_query, w_key, w_value, w_out, w_gate, w_up, w_down, q_gain, k_gain, attn_gain, mlp_gain):
    length = tokens.shape[0]
    query_raw = low_back(dense(tokens, w_query))
    key_raw = low_back(dense(tokens, w_key))
    value_raw = dense(tokens, w_value)
    query_norm = rms_norm(query_raw, q_gain)
    key_norm = rms_norm(key_raw, k_gain)
    cosine, sine = rope_tables(length)
    queries = low_back(low(rotate(query_norm.reshape(length, HEADS, HD), cosine, sine)))
    keys = low_back(low(rotate(key_norm.reshape(length, HEADS, HD), cosine, sine)))
    values = low_back(low(value_raw)).reshape(length, HEADS, HD)
    mixed = lax.map(jax.checkpoint(head_attend), (queries.transpose(1, 0, 2), keys.transpose(1, 0, 2), values.transpose(1, 0, 2)))
    mixed = low_back(low(mixed)).transpose(1, 0, 2).reshape(length, D)
    attn = low_back(dense(mixed, w_out))
    hidden_in = tokens + rms_norm(attn, attn_gain)
    hidden_low = low(hidden_in)
    gate = low_back(dense(hidden_low, w_gate))
    up_proj = low_back(dense(hidden_low, w_up))
    hidden = low(jax.nn.silu(gate) * up_proj)
    mlp = low_back(dense(hidden, w_down))
    return hidden_in + rms_norm(mlp, mlp_gain)

def reference(inputs, w_query, w_key, w_value, w_out, w_gate, w_up, w_down, q_gain, k_gain, attn_gain, mlp_gain, out_grad):
    params = tuple((p.astype(jnp.float32) for p in (w_query, w_key, w_value, w_out, w_gate, w_up, w_down, q_gain, k_gain, attn_gain, mlp_gain)))

    def step(totals, pair):
        tokens, cotangent = pair
        result, pull = jax.vjp(forward, tokens.astype(jnp.float32), *params)
        grads = pull(cotangent.astype(jnp.float32))
        totals = tuple((t + g for t, g in zip(totals, grads[1:])))
        return (totals, (result.astype(jnp.bfloat16), grads[0]))
    start = tuple((jnp.zeros(p.shape, jnp.float32) for p in params))
    totals, (outputs, input_grads) = lax.scan(step, start, (inputs, out_grad))
    return (outputs, input_grads, totals[0], totals[1], totals[2], totals[3], totals[4], totals[5], totals[6], totals[7], totals[8], totals[9], totals[10])
```

```python
import functools

import jax
import jax.numpy as jnp
from jax import lax
from jax.sharding import PartitionSpec as P

HD = 128


EPSILON = 1e-06
THETA = 500000.0


def product(left, right):
    return jnp.dot(left, right, preferred_element_type=jnp.float32)


def left_product(left, right):
    return lax.dot_general(
        left, right, (((0,), (0,)), ((), ())), preferred_element_type=jnp.float32
    )


def right_product(left, right):
    return lax.dot_general(
        left, right, (((1,), (1,)), ((), ())), preferred_element_type=jnp.float32
    )


def rope_tables(count, head_size, offset):
    half = head_size // 2
    freq = 1.0 / THETA ** (jnp.arange(half, dtype=jnp.float32) * 2.0 / head_size)
    where_at = (offset + jnp.arange(count)).astype(jnp.float32)
    angle = where_at[:, None] * freq[None, :]
    return (jnp.cos(angle)[:, None, :], jnp.sin(angle)[:, None, :])


def rotate(field, cosine, sine):
    half = field.shape[-1] // 2
    first = field[..., :half]
    second = field[..., half:]
    return jnp.concatenate(
        [first * cosine - second * sine, second * cosine + first * sine], axis=-1
    )


def norm_back(field, factor, gain, upstream):
    inner = jnp.mean(field * gain * upstream, axis=1, keepdims=True)
    return factor * (gain * upstream) - field * factor * factor * factor * inner


def attend_forward(queries, keys, values, scale):
    length, heads, head_size = queries.shape
    block = min(512, length)
    count = length // block
    columns = jnp.arange(length)[None, None, :]

    def one(items):
        query_block, start = items
        scores = (
            jnp.einsum("qhd,khd->hqk", query_block, keys, preferred_element_type=jnp.float32)
            * scale
        )
        places = start + jnp.arange(block)[None, :, None]
        scores = jnp.where(columns <= places, scores, -jnp.inf)
        peak = jnp.max(scores, axis=2, keepdims=True)
        expo = jnp.exp(scores - peak)
        total = jnp.sum(expo, axis=2, keepdims=True)
        probs = (expo / total).astype(jnp.bfloat16)
        mixed = jnp.einsum("hqk,khd->qhd", probs, values, preferred_element_type=jnp.float32)
        return (mixed.astype(jnp.bfloat16), (peak + jnp.log(total))[..., 0])

    mixed, logsum = lax.map(
        one, (queries.reshape(count, block, heads, head_size), jnp.arange(count) * block)
    )
    return (mixed.reshape(length, heads, head_size), logsum)


def attend_backward(queries, keys, values, upstream, logsum, scale):
    length, heads, head_size = queries.shape
    block = min(512, length)
    count = length // block
    columns = jnp.arange(length)[None, None, :]

    def one(carry, items):
        key_total, value_total = carry
        query_block, up_block, logsum_block, start = items
        scores = (
            jnp.einsum("qhd,khd->hqk", query_block, keys, preferred_element_type=jnp.float32)
            * scale
        )
        places = start + jnp.arange(block)[None, :, None]
        probs = jnp.where(columns <= places, jnp.exp(scores - logsum_block[..., None]), 0.0)
        prob_back = jnp.einsum("qhd,khd->hqk", up_block, values, preferred_element_type=jnp.float32)
        value_total = value_total + jnp.einsum(
            "hqk,qhd->khd", probs.astype(jnp.bfloat16), up_block, preferred_element_type=jnp.float32
        )
        delta = jnp.sum(prob_back * probs, axis=2, keepdims=True)
        score_back = (probs * (prob_back - delta)).astype(jnp.bfloat16)
        query_back = (
            jnp.einsum("hqk,khd->qhd", score_back, keys, preferred_element_type=jnp.float32) * scale
        )
        key_total = (
            key_total
            + jnp.einsum(
                "hqk,qhd->khd", score_back, query_block, preferred_element_type=jnp.float32
            )
            * scale
        )
        return ((key_total, value_total), query_back.astype(jnp.bfloat16))

    zeros = jnp.zeros((length, heads, head_size), jnp.float32)
    blocks = (
        queries.reshape(count, block, heads, head_size),
        upstream.reshape(count, block, heads, head_size),
        logsum,
        jnp.arange(count) * block,
    )
    (key_total, value_total), query_back = lax.scan(one, (zeros, zeros), blocks)
    return (
        query_back.reshape(length, heads, head_size),
        key_total.astype(jnp.bfloat16),
        value_total.astype(jnp.bfloat16),
    )


def ring_shift(size, step):
    return [(i, (i + step) % size) for i in range(size)]


def spun(field, place, parts, axis=0):
    rows = field.shape[axis] // parts
    return jnp.concatenate(
        [
            lax.dynamic_slice_in_dim(field, ((place + k) % parts) * rows, rows, axis)
            for k in range(parts)
        ],
        axis=axis,
    )


def small_sum(field, size):
    total = field
    for k in range(1, size):
        total = total + lax.ppermute(field, "tp", ring_shift(size, k))
    return total


def scatter_sum(partial, size):
    rows = partial.shape[0] // size
    total = partial[:rows]
    for k in range(1, size):
        piece = partial[k * rows : (k + 1) * rows].astype(jnp.bfloat16)
        total = total + lax.ppermute(piece, "tp", ring_shift(size, k)).astype(jnp.float32)
    return total


def gather(chunk, size):
    pieces = [chunk]
    for k in range(1, size):
        pieces.append(lax.ppermute(chunk, "tp", ring_shift(size, -k)))
    return jnp.concatenate(pieces, axis=0)


def shards(
    tp_size,
    inputs,
    w_query,
    w_key,
    w_value,
    w_out,
    w_gate,
    w_up,
    w_down,
    q_gain,
    k_gain,
    attn_gain,
    mlp_gain,
    out_grad,
):
    tokens = inputs[0]
    count, width = tokens.shape
    head_size = HD
    local_heads = w_query.shape[1] // head_size
    scale = HD ** (-0.5)
    place = lax.axis_index("tp")
    back = (tp_size - place) % tp_size
    rows = count // tp_size
    cosine, sine = rope_tables(count, head_size, lax.axis_index("sp") * count)
    tokens_own = lax.dynamic_slice_in_dim(tokens, place * rows, rows, 0).astype(jnp.float32)
    upstream = lax.dynamic_slice_in_dim(out_grad[0], place * rows, rows, 0).astype(jnp.float32)
    query_raw = product(tokens, w_query)
    key_raw = product(tokens, w_key)
    value_raw = product(tokens, w_value)
    squares = small_sum(
        jnp.stack([jnp.sum(query_raw * query_raw, axis=1), jnp.sum(key_raw * key_raw, axis=1)]),
        tp_size,
    )
    query_factor = lax.rsqrt(squares[0] / width + EPSILON)[:, None]
    key_factor = lax.rsqrt(squares[1] / width + EPSILON)[:, None]
    query_send = rotate(
        (query_raw * query_factor * q_gain).reshape(count, local_heads, head_size), cosine, sine
    ).astype(jnp.bfloat16)
    key_send = rotate(
        (key_raw * key_factor * k_gain).reshape(count, local_heads, head_size), cosine, sine
    ).astype(jnp.bfloat16)
    value_send = value_raw.astype(jnp.bfloat16).reshape(count, local_heads, head_size)
    queries, keys, values = (
        lax.all_to_all(query_send, "sp", split_axis=1, concat_axis=0, tiled=True),
        lax.all_to_all(key_send, "sp", split_axis=1, concat_axis=0, tiled=True),
        lax.all_to_all(value_send, "sp", split_axis=1, concat_axis=0, tiled=True),
    )
    mixed_heads, logsum = attend_forward(queries, keys, values, scale)
    mixed = lax.all_to_all(mixed_heads, "sp", split_axis=0, concat_axis=1, tiled=True).reshape(
        count, -1
    )
    mixed = spun(mixed, place, tp_size)
    attn = scatter_sum(product(mixed, w_out), tp_size)
    attn_factor = lax.rsqrt(jnp.mean(attn * attn, axis=1, keepdims=True) + EPSILON)
    hidden_in = tokens_own + attn * attn_factor * attn_gain
    hidden_low = gather(hidden_in.astype(jnp.bfloat16), tp_size)
    gate = product(hidden_low, w_gate)
    up_proj = product(hidden_low, w_up)
    sigmoid_gate = jax.nn.sigmoid(gate)
    hidden = (gate * sigmoid_gate * up_proj).astype(jnp.bfloat16)
    mlp = scatter_sum(product(hidden, w_down), tp_size)
    mlp_factor = lax.rsqrt(jnp.mean(mlp * mlp, axis=1, keepdims=True) + EPSILON)
    output_own = (hidden_in + mlp * mlp_factor * mlp_gain).astype(jnp.bfloat16)
    mlp_gain_part = jnp.sum(upstream * mlp * mlp_factor, axis=0)
    mlp_back = gather(norm_back(mlp, mlp_factor, mlp_gain, upstream).astype(jnp.bfloat16), tp_size)
    output = spun(gather(output_own, tp_size), back, tp_size)
    w_down_part = left_product(hidden, mlp_back).astype(jnp.bfloat16)
    hidden_back = right_product(mlp_back, w_down)
    up_back = (hidden_back * gate * sigmoid_gate).astype(jnp.bfloat16)
    gate_back = (hidden_back * up_proj * sigmoid_gate * (1.0 + gate * (1.0 - sigmoid_gate))).astype(
        jnp.bfloat16
    )
    w_gate_part = left_product(hidden_low, gate_back).astype(jnp.bfloat16)
    w_up_part = left_product(hidden_low, up_back).astype(jnp.bfloat16)
    residual_back = upstream + scatter_sum(
        right_product(gate_back, w_gate) + right_product(up_back, w_up), tp_size
    )
    attn_gain_part = jnp.sum(residual_back * attn * attn_factor, axis=0)
    attn_back = gather(
        norm_back(attn, attn_factor, attn_gain, residual_back).astype(jnp.bfloat16), tp_size
    )
    w_out_part = left_product(mixed, attn_back).astype(jnp.bfloat16)
    mixed_back = spun(right_product(attn_back, w_out).astype(jnp.bfloat16), back, tp_size).reshape(
        count, local_heads, head_size
    )
    heads_back = lax.all_to_all(mixed_back, "sp", split_axis=1, concat_axis=0, tiled=True)
    query_heads_back, key_heads_back, value_heads_back = attend_backward(
        queries, keys, values, heads_back, logsum, scale
    )
    query_back, key_back, value_back = (
        lax.all_to_all(query_heads_back, "sp", split_axis=0, concat_axis=1, tiled=True),
        lax.all_to_all(key_heads_back, "sp", split_axis=0, concat_axis=1, tiled=True),
        lax.all_to_all(value_heads_back, "sp", split_axis=0, concat_axis=1, tiled=True),
    )
    query_norm_back = rotate(query_back.astype(jnp.float32), cosine, -sine).reshape(count, -1)
    key_norm_back = rotate(key_back.astype(jnp.float32), cosine, -sine).reshape(count, -1)
    value_raw_back = value_back.reshape(count, -1)
    inners = small_sum(
        jnp.stack(
            [
                jnp.sum(query_raw * q_gain * query_norm_back, axis=1),
                jnp.sum(key_raw * k_gain * key_norm_back, axis=1),
            ]
        ),
        tp_size,
    )
    q_gain_part = jnp.sum(query_norm_back * query_raw * query_factor, axis=0)
    k_gain_part = jnp.sum(key_norm_back * key_raw * key_factor, axis=0)
    query_raw_back = (
        query_factor * (q_gain * query_norm_back)
        - query_raw * query_factor**3 * (inners[0] / width)[:, None]
    ).astype(jnp.bfloat16)
    key_raw_back = (
        key_factor * (k_gain * key_norm_back)
        - key_raw * key_factor**3 * (inners[1] / width)[:, None]
    ).astype(jnp.bfloat16)
    raw_back = jnp.concatenate([query_raw_back, key_raw_back, value_raw_back], axis=1)
    w_heads_part = left_product(tokens, raw_back).astype(jnp.bfloat16)
    spun_back = spun(raw_back, place, tp_size)
    columns = w_query.shape[1]
    projected = (
        right_product(spun_back[:, :columns], w_query)
        + right_product(spun_back[:, columns : 2 * columns], w_key)
        + right_product(spun_back[:, 2 * columns :], w_value)
    )
    input_own = residual_back + scatter_sum(projected, tp_size)
    input_grad = spun(gather(input_own.astype(jnp.bfloat16), tp_size), back, tp_size).astype(
        jnp.float32
    )
    gain_sums = lax.psum((q_gain_part, k_gain_part), ("dp", "sp"))
    post_sums = lax.psum((attn_gain_part, mlp_gain_part), ("dp", "sp", "tp"))
    slot = lax.axis_index(("dp", "sp"))
    share = width // lax.axis_size(("dp", "sp"))
    post_own = [lax.dynamic_slice_in_dim(v, slot * share, share, 0) for v in post_sums]

    def summed(part, dim):
        return lax.psum_scatter(part, ("dp", "sp"), scatter_dimension=dim, tiled=True).astype(
            jnp.float32
        )

    down_sum = summed(w_down_part, 1)
    gate_sum = summed(w_gate_part, 0)
    up_sum = summed(w_up_part, 0)
    out_sum = summed(w_out_part, 1)
    heads_sum = summed(w_heads_part, 0)
    return (
        output[None],
        input_grad[None],
        heads_sum[:, :columns],
        heads_sum[:, columns : 2 * columns],
        heads_sum[:, 2 * columns :],
        out_sum,
        gate_sum,
        up_sum,
        down_sum,
        gain_sums[0],
        gain_sums[1],
        post_own[0],
        post_own[1],
    )


def solution(mesh):
    in_specs = (
        P("dp", "sp", None),
        P(None, "tp"),
        P(None, "tp"),
        P(None, "tp"),
        P("tp", None),
        P(None, "tp"),
        P(None, "tp"),
        P("tp", None),
        P("tp"),
        P("tp"),
        P(),
        P(),
        P("dp", "sp", None),
    )
    out_specs = (
        P("dp", "sp", None),
        P("dp", "sp", None),
        P(("dp", "sp"), "tp"),
        P(("dp", "sp"), "tp"),
        P(("dp", "sp"), "tp"),
        P("tp", ("dp", "sp")),
        P(("dp", "sp"), "tp"),
        P(("dp", "sp"), "tp"),
        P("tp", ("dp", "sp")),
        P("tp"),
        P("tp"),
        P(("dp", "sp")),
        P(("dp", "sp")),
    )
    return jax.shard_map(functools.partial(shards, mesh.shape["tp"]), mesh=mesh, in_specs=in_specs, out_specs=out_specs, check_vma=False)
```

```python
import functools

import jax
import jax.numpy as jnp
from jax import lax
from jax.sharding import PartitionSpec as P

HD = 128


EPSILON = 1e-06
THETA = 500000.0


def product(left, right):
    return jnp.dot(left, right, preferred_element_type=jnp.float32)


def left_product(left, right):
    return lax.dot_general(
        left, right, (((0,), (0,)), ((), ())), preferred_element_type=jnp.float32
    )


def right_product(left, right):
    return lax.dot_general(
        left, right, (((1,), (1,)), ((), ())), preferred_element_type=jnp.float32
    )


def rotate(field, cosine, sine):
    half = field.shape[-1] // 2
    first = field[..., :half]
    second = field[..., half:]
    return jnp.concatenate(
        [first * cosine - second * sine, second * cosine + first * sine], axis=-1
    )


def norm_back(field, factor, gain, upstream):
    inner = jnp.mean(field * gain * upstream, axis=1, keepdims=True)
    return factor * (gain * upstream) - field * factor * factor * factor * inner


def attend_forward(queries, keys, values, scale, diagonal, parts):
    block = diagonal.shape[0]
    mixed = []
    logsums = []
    for b in range(parts):
        seen = b * block
        query_block = queries[seen : seen + block]
        scores = right_product(query_block, keys[: seen + block]) * scale
        if b:
            allowed = jnp.concatenate([jnp.ones((block, seen), jnp.bool_), diagonal], axis=1)
        else:
            allowed = diagonal
        scores = jnp.where(allowed, scores, -jnp.inf)
        peak = jnp.max(scores, axis=1, keepdims=True)
        expo = jnp.exp(scores - peak)
        total = jnp.sum(expo, axis=1, keepdims=True)
        probs = (expo / total).astype(jnp.bfloat16)
        mixed.append(product(probs, values[: seen + block]).astype(jnp.bfloat16))
        logsums.append(peak + jnp.log(total))
    return mixed, logsums


def attend_backward(queries, keys, values, upstream, logsums, scale, diagonal, parts):
    block = diagonal.shape[0]
    query_back = []
    key_total = [0.0] * parts
    value_total = [0.0] * parts
    for b in range(parts):
        seen = b * block
        query_block = queries[seen : seen + block]
        up_block = upstream[seen : seen + block]
        scores = right_product(query_block, keys[: seen + block]) * scale
        if b:
            allowed = jnp.concatenate([jnp.ones((block, seen), jnp.bool_), diagonal], axis=1)
        else:
            allowed = diagonal
        probs = jnp.where(allowed, jnp.exp(scores - logsums[b]), 0.0)
        prob_back = right_product(up_block, values[: seen + block])
        value_part = left_product(probs.astype(jnp.bfloat16), up_block)
        delta = jnp.sum(prob_back * probs, axis=1, keepdims=True)
        score_back = (probs * (prob_back - delta)).astype(jnp.bfloat16)
        query_back.append(
            (product(score_back, keys[: seen + block]) * scale).astype(jnp.bfloat16)
        )
        key_part = left_product(score_back, query_block) * scale
        for k in range(b + 1):
            rows = slice(k * block, (k + 1) * block)
            key_total[k] = key_total[k] + key_part[rows]
            value_total[k] = value_total[k] + value_part[rows]
    return (
        query_back,
        [total.astype(jnp.bfloat16) for total in key_total],
        [total.astype(jnp.bfloat16) for total in value_total],
    )


def ring_shift(size, step):
    return [(i, (i + step) % size) for i in range(size)]


def flip(size, bit):
    return [(i, i ^ bit) for i in range(size)]


def spun(field, place, parts, axis=0):
    rows = field.shape[axis] // parts
    return jnp.concatenate(
        [
            lax.dynamic_slice_in_dim(field, ((place + k) % parts) * rows, rows, axis)
            for k in range(parts)
        ],
        axis=axis,
    )


def small_sum(field, size):
    total = field
    for k in range(1, size):
        total = total + lax.ppermute(field, "tp", ring_shift(size, k))
    return total


def token_sum(field, size):
    total = field
    rows = field.shape[1] // size
    for k in range(1, size):
        received = lax.ppermute(field, "tp", ring_shift(size, k))
        total = total + jnp.roll(received, -k * rows, axis=1)
    return total


def scatter_sum(partial, size, place):
    rows = partial.shape[0] // size
    pieces = [partial[k * rows : (k + 1) * rows] for k in range(size)]
    if size == 4:
        far = jnp.where(place == 0, pieces[3], pieces[1])
        relay = lax.ppermute(far, "tp", [(0, 1), (3, 2)])
        near = lax.ppermute(pieces[1], "tp", [(0, 1), (1, 2), (2, 3)])
        other = lax.ppermute(pieces[3], "tp", [(1, 0), (2, 1), (3, 2)])
        middle = (pieces[2].astype(jnp.float32) + relay.astype(jnp.float32)).astype(jnp.bfloat16)
        across = lax.ppermute(middle, "tp", ring_shift(4, 2))
        received = [near, other, across]
    else:
        received = [
            lax.ppermute(pieces[k], "tp", ring_shift(size, k)) for k in range(1, size)
        ]
    total = pieces[0].astype(jnp.float32)
    for piece in received:
        total = total + piece.astype(jnp.float32)
    return total


def gather(chunk, size, place):
    if size == 4:
        across = lax.ppermute(chunk, "tp", ring_shift(4, 2))
        near = lax.ppermute(chunk, "tp", [(0, 1), (1, 2), (2, 3)])
        other = lax.ppermute(chunk, "tp", [(1, 0), (2, 1), (3, 2)])
        relay = lax.ppermute(across, "tp", [(1, 0), (2, 3)])
        before = jnp.where(place == 0, relay, near)
        after = jnp.where(place == 3, relay, other)
        return jnp.concatenate([chunk, after, across, before], axis=0)
    pieces = [chunk]
    for k in range(1, size):
        pieces.append(lax.ppermute(chunk, "tp", ring_shift(size, -k)))
    return jnp.concatenate(pieces, axis=0)


def to_heads(pieces, place, size):
    received = [pieces[0]] + [
        lax.ppermute(pieces[k], "sp", flip(size, k)) for k in range(1, size)
    ]
    stacked = jnp.stack(received)
    return [lax.dynamic_index_in_dim(stacked, b ^ place, 0, keepdims=False) for b in range(size)]


def from_heads(blocks, place, size):
    stacked = jnp.stack(blocks)
    pieces = [
        lax.dynamic_index_in_dim(stacked, k ^ place, 0, keepdims=False) for k in range(size)
    ]
    received = [pieces[0]] + [
        lax.ppermute(pieces[k], "sp", flip(size, k)) for k in range(1, size)
    ]
    return received


def dp_order(size, index):
    return [1 - index, index] if size == 2 else list(range(size))


def dp_reduce(blocks, size):
    if size == 2:
        received = lax.ppermute(blocks[0].astype(jnp.bfloat16), "dp", [(0, 1), (1, 0)])
        return blocks[1].astype(jnp.float32) + received.astype(jnp.float32)
    stacked = jnp.stack([block.astype(jnp.bfloat16) for block in blocks])
    return lax.psum_scatter(stacked, "dp", scatter_dimension=0).astype(jnp.float32)


def sp_reduce(blocks, size):
    received = lax.ppermute(blocks[0].astype(jnp.bfloat16), "sp", flip(size, 2))
    return blocks[1].astype(jnp.float32) + received.astype(jnp.float32)


def group_sum(field, dp_size, sp_size):
    for bit in (1, 2):
        field = field + lax.ppermute(field, "sp", flip(sp_size, bit))
    if dp_size == 2:
        return field + lax.ppermute(field, "dp", [(0, 1), (1, 0)])
    return lax.psum(field, "dp")


def shards(
    sizes,
    inputs,
    w_query,
    w_key,
    w_value,
    w_out,
    w_gate,
    w_up,
    w_down,
    q_gain,
    k_gain,
    attn_gain,
    mlp_gain,
    out_grad,
):
    dp_size, sp_size, tp_size = sizes
    count, width = inputs.shape[1:]
    head_size = HD
    local_heads = w_query.shape[1] // head_size
    held = local_heads // sp_size
    scale = HD ** (-0.5)
    place = lax.axis_index("tp")
    seat = lax.axis_index("sp")
    rank = lax.axis_index("dp")
    core = seat % 2
    side = seat // 2
    back = (tp_size - place) % tp_size
    rows = count // tp_size
    share = width // (dp_size * sp_size)
    columns = w_query.shape[1]

    def chosen(field, which):
        picks = []
        for d in dp_order(dp_size, rank):
            for y in (1 - side, side):
                slot = (d * 2 + y) * 2 + which
                picks.append(lax.dynamic_slice_in_dim(field, slot * share, share, 1))
        return jnp.concatenate(picks, axis=1)

    def swapped(field):
        return lax.ppermute(field, "sp", flip(sp_size, 1))

    def joined(field):
        return jnp.concatenate([field, swapped(field)], axis=0)

    def joined_chosen(field):
        return jnp.concatenate([chosen(field, core), swapped(chosen(field, 1 - core))], axis=0)

    def other_dp(field):
        return [field[:, d * 2 * share : (d + 1) * 2 * share] for d in range(dp_size)]

    def other_sp(field):
        return [
            jnp.concatenate(
                [
                    field[:, (d * 2 + y) * share : (d * 2 + y + 1) * share]
                    for d in range(dp_size)
                ],
                axis=1,
            )
            for y in range(2)
        ]

    def summed(first, second, field, along):
        def outer(split, whole):
            if along == 0:
                return left_product(split, whole).astype(jnp.bfloat16)
            return left_product(whole, split).astype(jnp.bfloat16)

        def cut(block, index, parts):
            size = block.shape[along] // parts
            return lax.slice_in_dim(block, index * size, (index + 1) * size, axis=along)

        dp_first = dp_reduce([outer(part, first) for part in other_dp(field)], dp_size)
        sp_first = sp_reduce([outer(part, second) for part in other_sp(field)], sp_size)
        dp_then = sp_reduce([cut(dp_first, y, 2) for y in range(2)], sp_size)
        sp_then = dp_reduce([cut(sp_first, d, dp_size) for d in range(dp_size)], dp_size)
        return dp_then, sp_then

    where_in = (place * rows + jnp.arange(count)) % count
    diagonal = where_in[None, :] <= where_in[:, None]
    tokens = spun(inputs[0], place, tp_size)
    upstream = spun(out_grad[0], place, tp_size).astype(jnp.float32)
    half = head_size // 2
    freq = 1.0 / THETA ** (jnp.arange(half, dtype=jnp.float32) * 2.0 / head_size)
    angle = (seat * count + where_in).astype(jnp.float32)[:, None] * freq[None, :]
    cosine = jnp.cos(angle)[:, None, :]
    sine = jnp.sin(angle)[:, None, :]

    query_raw = product(tokens, w_query)
    key_raw = product(tokens, w_key)
    value_raw = product(tokens, w_value)
    squares = token_sum(
        jnp.stack([jnp.sum(query_raw * query_raw, axis=1), jnp.sum(key_raw * key_raw, axis=1)]),
        tp_size,
    )
    query_factor = lax.rsqrt(squares[0] / width + EPSILON)[:, None]
    key_factor = lax.rsqrt(squares[1] / width + EPSILON)[:, None]
    query_send = rotate(
        (query_raw * query_factor * q_gain).reshape(count, local_heads, head_size), cosine, sine
    ).astype(jnp.bfloat16)
    key_send = rotate(
        (key_raw * key_factor * k_gain).reshape(count, local_heads, head_size), cosine, sine
    ).astype(jnp.bfloat16)
    span = held * head_size

    def for_seat(field, k):
        return lax.dynamic_slice_in_dim(field, (seat ^ k) * span, span, 1)

    flat = [
        query_send.reshape(count, columns),
        key_send.reshape(count, columns),
        value_raw.astype(jnp.bfloat16),
    ]
    arrived = to_heads(
        [
            jnp.concatenate([for_seat(field, k) for field in flat], axis=1)
            for k in range(sp_size)
        ],
        seat,
        sp_size,
    )
    whole = jnp.concatenate(arrived, axis=0)

    def head(field, kind, h):
        at = kind * span + h * head_size
        return field[:, at : at + head_size]

    kept = []
    for h in range(held):
        queries, keys, values = (head(whole, kind, h) for kind in range(3))
        mixed_blocks, logsums = attend_forward(queries, keys, values, scale, diagonal, sp_size)
        kept.append((queries, keys, values, logsums, mixed_blocks))
    mixed_blocks = [
        jnp.concatenate([item[4][b] for item in kept], axis=1) for b in range(sp_size)
    ]

    def by_seat(pieces):
        stacked = jnp.stack(pieces)
        return jnp.concatenate(
            [
                lax.dynamic_index_in_dim(stacked, s ^ seat, 0, keepdims=False)
                for s in range(sp_size)
            ],
            axis=1,
        )

    mixed = by_seat(from_heads(mixed_blocks, seat, sp_size))
    attn = scatter_sum(product(mixed, w_out).astype(jnp.bfloat16), tp_size, place)
    attn_factor = lax.rsqrt(jnp.mean(attn * attn, axis=1, keepdims=True) + EPSILON)
    hidden_in = tokens[:rows].astype(jnp.float32) + attn * attn_factor * attn_gain
    hidden_low = gather(hidden_in.astype(jnp.bfloat16), tp_size, place)
    gate = product(hidden_low, w_gate)
    up_proj = product(hidden_low, w_up)
    sigmoid_gate = jax.nn.sigmoid(gate)
    hidden = (gate * sigmoid_gate * up_proj).astype(jnp.bfloat16)
    mlp_own = scatter_sum(product(hidden, w_down).astype(jnp.bfloat16), tp_size, place)
    mlp = gather(mlp_own.astype(jnp.bfloat16), tp_size, place).astype(jnp.float32)
    mlp_factor = lax.rsqrt(jnp.mean(mlp * mlp, axis=1, keepdims=True) + EPSILON)
    mlp_back = norm_back(mlp, mlp_factor, mlp_gain, upstream).astype(jnp.bfloat16)
    output = spun(
        (hidden_low.astype(jnp.float32) + mlp * mlp_factor * mlp_gain).astype(jnp.bfloat16),
        back,
        tp_size,
    )
    mlp_gain_part = jnp.sum(upstream * mlp * mlp_factor, axis=0)
    hidden_back = right_product(mlp_back, w_down)
    up_back = (hidden_back * gate * sigmoid_gate).astype(jnp.bfloat16)
    gate_back = (hidden_back * up_proj * sigmoid_gate * (1.0 + gate * (1.0 - sigmoid_gate))).astype(
        jnp.bfloat16
    )
    residual_back = upstream[:rows] + scatter_sum(
        (right_product(gate_back, w_gate) + right_product(up_back, w_up)).astype(jnp.bfloat16),
        tp_size,
        place,
    )
    hidden_both = joined(hidden)
    inner = w_gate.shape[1] // 2
    down_sum = jnp.concatenate(
        summed(
            hidden_both[:, :inner], hidden_both[:, inner:], joined_chosen(mlp_back), 1
        ),
        axis=0,
    )
    gate_sum, up_sum = summed(joined(gate_back), joined(up_back), joined_chosen(hidden_low), 0)
    attn_gain_part = jnp.sum(residual_back * attn * attn_factor, axis=0)
    attn_back = gather(
        norm_back(attn, attn_factor, attn_gain, residual_back).astype(jnp.bfloat16), tp_size, place
    )
    mixed_back = right_product(attn_back, w_out).astype(jnp.bfloat16)
    heads_back = jnp.concatenate(
        to_heads([for_seat(mixed_back, k) for k in range(sp_size)], seat, sp_size), axis=0
    )
    backs = []
    for h in range(held):
        queries, keys, values, logsums, _ = kept[h]
        backs.append(
            attend_backward(
                queries,
                keys,
                values,
                head(heads_back, 0, h),
                logsums,
                scale,
                diagonal,
                sp_size,
            )
        )
    returned = from_heads(
        [
            jnp.concatenate(
                [backs[h][kind][b] for kind in range(3) for h in range(held)], axis=1
            )
            for b in range(sp_size)
        ],
        seat,
        sp_size,
    )
    query_back, key_back, value_raw_back = (
        by_seat([piece[:, kind * span : (kind + 1) * span] for piece in returned])
        for kind in range(3)
    )
    mixed_both = joined(mixed)
    out_sum = jnp.concatenate(
        summed(
            mixed_both[:, : columns // 2],
            mixed_both[:, columns // 2 :],
            joined_chosen(attn_back),
            1,
        ),
        axis=0,
    )
    query_norm_back = rotate(
        query_back.astype(jnp.float32).reshape(count, local_heads, head_size), cosine, -sine
    ).reshape(count, -1)
    key_norm_back = rotate(
        key_back.astype(jnp.float32).reshape(count, local_heads, head_size), cosine, -sine
    ).reshape(count, -1)
    inners = token_sum(
        jnp.stack(
            [
                jnp.sum(query_raw * q_gain * query_norm_back, axis=1),
                jnp.sum(key_raw * k_gain * key_norm_back, axis=1),
            ]
        ),
        tp_size,
    )
    q_gain_part = jnp.sum(query_norm_back * query_raw * query_factor, axis=0)
    k_gain_part = jnp.sum(key_norm_back * key_raw * key_factor, axis=0)
    query_raw_back = (
        query_factor * (q_gain * query_norm_back)
        - query_raw * query_factor**3 * (inners[0] / width)[:, None]
    ).astype(jnp.bfloat16)
    key_raw_back = (
        key_factor * (k_gain * key_norm_back)
        - key_raw * key_factor**3 * (inners[1] / width)[:, None]
    ).astype(jnp.bfloat16)
    projected = (
        right_product(query_raw_back, w_query)
        + right_product(key_raw_back, w_key)
        + right_product(value_raw_back, w_value)
    )
    input_own = residual_back + scatter_sum(projected.astype(jnp.bfloat16), tp_size, place)
    input_grad = spun(gather(input_own.astype(jnp.bfloat16), tp_size, place), back, tp_size).astype(
        jnp.float32
    )
    raw_back = jnp.concatenate([query_raw_back, key_raw_back, value_raw_back], axis=1)
    raw_both = joined(raw_back)
    middle = raw_back.shape[1] // 2
    heads_sum = jnp.concatenate(
        summed(raw_both[:, :middle], raw_both[:, middle:], joined_chosen(tokens), 0), axis=1
    )
    post_sums = group_sum(
        jnp.stack([small_sum(attn_gain_part, tp_size), mlp_gain_part]), dp_size, sp_size
    )
    gain_sums = group_sum(jnp.stack([q_gain_part, k_gain_part]), dp_size, sp_size)
    slot = rank * sp_size + seat
    post_own = lax.dynamic_slice_in_dim(post_sums, slot * share, share, 1)
    return (
        output[None],
        input_grad[None],
        heads_sum[:, :columns],
        heads_sum[:, columns : 2 * columns],
        heads_sum[:, 2 * columns :],
        out_sum,
        gate_sum,
        up_sum,
        down_sum,
        gain_sums[0],
        gain_sums[1],
        post_own[0],
        post_own[1],
    )


def solution(mesh):
    in_specs = (
        P("dp", "sp", None),
        P(None, "tp"),
        P(None, "tp"),
        P(None, "tp"),
        P("tp", None),
        P(None, "tp"),
        P(None, "tp"),
        P("tp", None),
        P("tp"),
        P("tp"),
        P(),
        P(),
        P("dp", "sp", None),
    )
    out_specs = (
        P("dp", "sp", None),
        P("dp", "sp", None),
        P(("dp", "sp"), "tp"),
        P(("dp", "sp"), "tp"),
        P(("dp", "sp"), "tp"),
        P("tp", ("dp", "sp")),
        P(("dp", "sp"), "tp"),
        P(("dp", "sp"), "tp"),
        P("tp", ("dp", "sp")),
        P("tp"),
        P("tp"),
        P(("dp", "sp")),
        P(("dp", "sp")),
    )
    sizes = tuple(mesh.shape[axis] for axis in ("dp", "sp", "tp"))
    return jax.shard_map(
        functools.partial(shards, sizes),
        mesh=mesh,
        in_specs=in_specs,
        out_specs=out_specs,
        check_vma=False,
    )
```
